32 devices in a mesh: col: 8 (over z, core), row: 4 (over y, x).
Axes of the slice: x: 2, y: 2, z: 4, core: 2. Of those that a mesh axis runs over, the one named last changes fastest.
Arguments:
- matrix: float32 [4096, 4096], P('row', 'col'), may hold values from -64 to 64, as said below
- plan: int32 [3, 8], replicated, may hold values from 0 to 1
Outputs:
- rotated: float32 [4096, 4096], P('row', 'col')
- coupling: float32 [3], replicated
The draws below stay inside these ranges and needn't reach their ends.
Inputs may be any that keep to these rules, and one draw needn't show every extreme that they name: Entries of the matrix are real numbers; column scales differ between columns.
All inputs are finite; a program needn't handle non-finite values.
Results may differ from the reference program's by a relative error of at most 0.0003.
Values sent between devices are 32-bit elements; how exact they have to be, the bound alone decides.
A program may use at most 128 MiB of HBM per device.

```python
import jax
import jax.numpy as jnp
from jax import lax

BLOCK = 256
SWEEPS = 2
STEPS = 3
ROWS = 4096
COLS = 4096
N_COL = 8


def draw_matrix(key, part):
    key_base = jax.random.fold_in(key, 11)
    key_cols = jax.random.fold_in(key, 12)
    column = jnp.arange(COLS).astype(jnp.float32)
    rising = 1.0 + 3.0 * column / COLS
    rough = jnp.exp(jax.random.uniform(key_cols, (COLS,), jnp.float32, -0.7, 0.7))
    base = jnp.clip(jax.random.normal(key_base, (ROWS, COLS), jnp.float32), -6.0, 6.0)
    values = base * (rough * rising)[None, :]
    return jnp.clip(values, -64.0, 64.0)


def set_ends(array, key, least, largest):
    index_at = [jax.random.randint(jax.random.fold_in(key, axis), (), 0, length) for axis, length in enumerate(array.shape)]
    longest = array.shape.index(max(array.shape))
    neighbour = index_at[:longest] + [(index_at[longest] + 1) % array.shape[longest]] + index_at[longest + 1:]
    return array.at[tuple(index_at)].set(least).at[tuple(neighbour)].set(largest)


def setup_inputs(seed: int = 0) -> dict:
    key_list = jax.random.split(jax.random.key(seed), 3)
    return {
        "matrix": draw_matrix(jax.random.fold_in(key_list[2], 71), 0),
        "plan": set_ends(jax.random.randint(key_list[1], (STEPS, N_COL), 0, 2), jax.random.fold_in(key_list[1], 1), 0, 1).astype(jnp.int32),
    }


highest = lax.Precision.HIGHEST
eps = 1e-06

def product(first, second):
    return jnp.dot(first, second, precision=highest, preferred_element_type=jnp.float32)

def sweep_rotation(gram):
    width = gram.shape[0]
    eye = jnp.eye(width, dtype=jnp.float32)
    upper = jnp.triu(jnp.ones((width, width), jnp.float32), 1)
    rotation = eye
    for sweep in range(SWEEPS):
        diag = jnp.diagonal(gram)
        ratio = gram / (diag[:, None] + diag[None, :] + eps) * upper
        skew_raw = ratio - ratio.T
        scale = jnp.maximum(jnp.sqrt(jnp.sum(skew_raw * skew_raw)), 1.0)
        skew = skew_raw / scale
        square = product(skew, skew)
        system = eye - square
        inverse = 4.0 / 3.0 * eye - 4.0 / 9.0 * system
        for turn in range(2):
            inverse = product(inverse, 2.0 * eye - product(system, inverse))
        qmat = product(eye - 2.0 * skew + square, inverse)
        gram = product(qmat.T, product(gram, qmat))
        if sweep == 0:
            rotation = qmat
        else:
            rotation = product(rotation, qmat)
    return (rotation, gram)

def rotate_pair(pair):
    gram = lax.dot_general(pair, pair, (((0,), (0,)), ((), ())), precision=highest, preferred_element_type=jnp.float32)
    rotation, turned = sweep_rotation(gram)
    moved = product(pair, rotation)
    cross_sq = jnp.sum(turned[:BLOCK, BLOCK:] * turned[:BLOCK, BLOCK:])
    diag_sq = jnp.sum(jnp.diagonal(turned) ** 2)
    return (moved, cross_sq, diag_sq)

def reference(matrix, plan):
    pairs = matrix.reshape(ROWS, N_COL, 2 * BLOCK).transpose(1, 0, 2)
    values = []
    for step in range(STEPS):
        moved, cross_sq, diag_sq = lax.map(rotate_pair, pairs)
        values.append(jnp.log(jnp.sum(cross_sq) / jnp.sum(diag_sq)))
        left = moved[:, :, :BLOCK]
        right = moved[:, :, BLOCK:]
        flag = (plan[step] == 1)[:, None, None]
        send = jnp.where(flag, right, left)
        keep = jnp.where(flag, left, right)
        received = jnp.roll(send, 1, axis=0)
        pairs = jnp.concatenate([keep, received], axis=2)
    rotated = pairs.transpose(1, 0, 2).reshape(ROWS, COLS)
    return (rotated, jnp.stack(values).astype(jnp.float32))
```

```python
import functools

import jax
import jax.numpy as jnp
from jax import lax
from jax.experimental import pallas as pl
from jax.experimental.pallas import tpu as pltpu
from jax.sharding import PartitionSpec as P

SWEEPS = 2
STEPS = 3
MESH = pl.DeviceIdType.MESH
f32 = jnp.float32
bf16 = jnp.bfloat16
high = lax.Precision.HIGH
eps = 1e-06
COEF = tuple(c / 6561.0 for c in (6560.0, 6544.0, 6432.0, 5984.0, 4864.0, 3072.0, 1280.0, 256.0))


def split(x):
    big = x.astype(bf16)
    return big, (x - big.astype(f32)).astype(bf16)


def dot1(a, b):
    return jnp.dot(a, b, preferred_element_type=f32)


def dot3(a, b):
    return dot1(a[0], b[0]) + (dot1(a[0], b[1]) + dot1(a[1], b[0]))


def sweep(gram, row, column):
    on_diag = row == column
    only = jnp.where(on_diag, gram, 0.0)
    d_row = jnp.sum(only, axis=0, keepdims=True)
    d_col = jnp.sum(only, axis=1, keepdims=True)
    ratio = gram / (d_col + d_row + eps)
    raw = jnp.where(row < column, ratio, jnp.where(row > column, -ratio, 0.0))
    scale = jnp.maximum(jnp.sqrt(jnp.sum(raw * raw, keepdims=True)), 1.0)
    skew = raw / scale
    parts = split(skew)
    a1 = dot3(parts, parts)
    a1b = a1.astype(bf16)
    a2 = dot1(a1b, a1b)
    a2b = a2.astype(bf16)
    a3 = dot1(a1b, a2b)
    a4 = dot1(a2b, a2b)
    low = COEF[5] * a1 + COEF[6] * a2 + COEF[7] * a3
    tail = dot1(a4.astype(bf16), low.astype(bf16))
    above = COEF[1] * a1 + COEF[2] * a2 + COEF[3] * a3 + (COEF[4] * a4 + tail)
    factor = a1 - 2.0 * skew
    extra = above + COEF[0] * factor + dot1(factor.astype(bf16), above.astype(bf16))
    extra = extra + jnp.where(on_diag, COEF[0] - 1.0, 0.0)
    part = split(extra)
    half = gram + dot3(split(gram), part)
    turn = extra.T
    turned = half + dot3(split(turn), split(half))
    return extra, part, turned


def rotate_kernel(flag_ref, top_ref, cross_ref, low_ref, vs_ref, vk_ref, gs_ref, gk_ref, stat_ref, g_ref):
    block = top_ref.shape[0]
    width = 2 * block
    g_ref[:block, :block] = top_ref[...]
    g_ref[:block, block:] = cross_ref[...]
    g_ref[block:, :block] = cross_ref[...].T
    g_ref[block:, block:] = low_ref[...]
    row = lax.broadcasted_iota(jnp.int32, (width, width), 0)
    column = lax.broadcasted_iota(jnp.int32, (width, width), 1)
    total = None
    for turn in range(SWEEPS):
        extra, part, turned = sweep(g_ref[...], row, column)
        if total is None:
            total, total_part = extra, part
        else:
            total = total + extra + dot3(total_part, part)
            total_part = split(total)
        g_ref[...] = turned
    rotation = total + jnp.where(row == column, 1.0, 0.0)
    flag = flag_ref[0] == 1
    left = rotation[:, :block]
    right = rotation[:, block:]
    vs_ref[...] = jnp.where(flag, right, left)
    vk_ref[...] = jnp.where(flag, left, right)
    top = g_ref[:block, :block]
    low = g_ref[block:, block:]
    gs_ref[...] = jnp.where(flag, low, top)
    gk_ref[...] = jnp.where(flag, top, low)
    off = g_ref[:block, block:]
    cross_sq = jnp.sum(off * off)
    only = jnp.where(row == column, g_ref[...], 0.0)
    diag_sq = jnp.sum(only * only)
    lane = lax.broadcasted_iota(jnp.int32, stat_ref.shape, 1)
    stat_ref[...] = jnp.where(lane == 0, cross_sq, jnp.where(lane == 1, diag_sq, 0.0))


def rotate(flag, top, cross, low):
    block = top.shape[0]
    width = 2 * block
    vmem = pl.BlockSpec(memory_space=pltpu.VMEM)
    shape = jax.ShapeDtypeStruct
    return pl.pallas_call(
        rotate_kernel,
        out_shape=(
            shape((width, block), f32),
            shape((width, block), f32),
            shape((block, block), f32),
            shape((block, block), f32),
            shape((8, 128), f32),
        ),
        in_specs=[pl.BlockSpec(memory_space=pltpu.SMEM), vmem, vmem, vmem],
        out_specs=(vmem,) * 5,
        scratch_shapes=[pltpu.VMEM((width, width), f32)],
        compiler_params=pltpu.CompilerParams(vmem_limit_bytes=40 * 1024 * 1024),
        name="rotate",
    )(flag, top, cross, low)


def greet(axis, count, me):
    barrier = pltpu.get_barrier_semaphore()
    for k in range(1, count):
        pl.semaphore_signal(
            barrier, inc=1, device_id={axis: lax.rem(me + k, count)}, device_id_type=MESH
        )
    pl.semaphore_wait(barrier, count - 1)


def sum_kernel(axis, count, x_ref, out_ref, got, send_a, recv_a, send_b, recv_b):
    me = lax.axis_index(axis)
    rows = x_ref.shape[0] // count
    greet(axis, count, me)
    mine = pl.ds(pl.multiple_of(me * rows, rows), rows)
    copies = []
    for k in range(1, count):
        peer = lax.rem(me + k, count)
        theirs = pl.ds(pl.multiple_of(peer * rows, rows), rows)
        copy = pltpu.make_async_remote_copy(
            src_ref=x_ref.at[theirs],
            dst_ref=got.at[k - 1],
            send_sem=send_a.at[k - 1],
            recv_sem=recv_a.at[k - 1],
            device_id={axis: peer},
            device_id_type=MESH,
        )
        copy.start()
        copies.append(copy)
    for copy in copies:
        copy.wait()
    total = x_ref[mine, :]
    for k in range(1, count):
        total = total + got[k - 1]
    out_ref[mine, :] = total
    copies = []
    for k in range(1, count):
        peer = lax.rem(me + k, count)
        copy = pltpu.make_async_remote_copy(
            src_ref=out_ref.at[mine],
            dst_ref=out_ref.at[mine],
            send_sem=send_b.at[k - 1],
            recv_sem=recv_b.at[k - 1],
            device_id={axis: peer},
            device_id_type=MESH,
        )
        copy.start()
        copies.append(copy)
    for copy in copies:
        copy.wait()


def sum_over(x, axis, number):
    count = lax.axis_size(axis)
    rows, width = x.shape
    vmem = pl.BlockSpec(memory_space=pltpu.VMEM)
    return pl.pallas_call(
        functools.partial(sum_kernel, axis, count),
        out_shape=jax.ShapeDtypeStruct((rows, width), f32),
        in_specs=[vmem],
        out_specs=vmem,
        scratch_shapes=[pltpu.VMEM((count - 1, rows // count, width), f32)]
        + [pltpu.SemaphoreType.DMA((count - 1,))] * 4,
        compiler_params=pltpu.CompilerParams(
            collective_id=number, has_side_effects=True, vmem_limit_bytes=16 * 1024 * 1024
        ),
        name="row_sum",
    )(x)


def tally_kernel(axis, count, x_ref, out_ref, got, send, recv):
    me = lax.axis_index(axis)
    greet(axis, count, me)
    copies = []
    for k in range(1, count):
        copy = pltpu.make_async_remote_copy(
            src_ref=x_ref,
            dst_ref=got.at[me],
            send_sem=send.at[k - 1],
            recv_sem=recv.at[k - 1],
            device_id={axis: lax.rem(me + k, count)},
            device_id_type=MESH,
        )
        copy.start()
        copies.append(copy)
    got[me] = x_ref[...]
    for copy in copies:
        copy.wait()
    total = got[0]
    for k in range(1, count):
        total = total + got[k]
    out_ref[...] = total


def tally(x, axis, number):
    count = lax.axis_size(axis)
    vmem = pl.BlockSpec(memory_space=pltpu.VMEM)
    return pl.pallas_call(
        functools.partial(tally_kernel, axis, count),
        out_shape=jax.ShapeDtypeStruct(x.shape, f32),
        in_specs=[vmem],
        out_specs=vmem,
        scratch_shapes=[pltpu.VMEM((count,) + x.shape, f32)]
        + [pltpu.SemaphoreType.DMA((count - 1,))] * 2,
        compiler_params=pltpu.CompilerParams(
            collective_id=number, has_side_effects=True, vmem_limit_bytes=16 * 1024 * 1024
        ),
        name="tally",
    )(x)


def from_behind(x, axis, by):
    count = lax.axis_size(axis)
    return lax.ppermute(x, axis, [(i, (i + by) % count) for i in range(count)])


def product(first, second):
    return jnp.dot(first, second, precision=high, preferred_element_type=f32)


def local_product(first, second):
    return lax.dot_general(
        first, second, (((0,), (0,)), ((), ())), precision=high, preferred_element_type=f32
    )


def on_device(matrix, plan):
    block = matrix.shape[1] // 2
    position = lax.axis_index("col")
    picker = jnp.arange(plan.shape[1], dtype=jnp.int32) == position
    flags = jnp.sum(jnp.where(picker[None, :], plan, 0), axis=1)
    keep, received = matrix[:, :block], matrix[:, block:]
    upper = local_product(keep, matrix)
    lower = local_product(received, received)
    packed = sum_over(jnp.concatenate([upper[:, :block], upper[:, block:], lower], axis=0), "row", 0)
    top, cross, low = packed[:block], packed[block : 2 * block], packed[2 * block :]
    pair = matrix
    stats = []
    for step in range(STEPS):
        vs, vk, gs, gk, stat = rotate(flags[step : step + 1], top, cross, low)
        stats.append(stat[:1])
        send = product(pair, vs)
        if step + 1 < STEPS:
            received, low = from_behind((send, gs), "col", 1)
            top = gk
            keep = product(pair, vk)
            cross = sum_over(local_product(keep, received), "row", step + 1)
        else:
            received = from_behind(send, "col", 1)
            keep = product(pair, vk)
        pair = jnp.concatenate([keep, received], axis=1)
    tile = jnp.concatenate(stats + [jnp.zeros((8 - STEPS, 128), f32)], axis=0)
    summed = tally(tile, "col", STEPS)
    return (pair, jnp.log(summed[:STEPS, 0] / summed[:STEPS, 1]))


def solution(mesh):
    in_specs = (P("row", "col"), P())
    out_specs = (P("row", "col"), P())
    return jax.shard_map(
        on_device, mesh=mesh, in_specs=in_specs, out_specs=out_specs, check_vma=False
    )
```

```python
import functools

import jax
import jax.numpy as jnp
from jax import lax
from jax.experimental import pallas as pl
from jax.experimental.pallas import tpu as pltpu
from jax.sharding import PartitionSpec as P

SWEEPS = 2
STEPS = 3
MESH = pl.DeviceIdType.MESH
f32 = jnp.float32
bf16 = jnp.bfloat16
high = lax.Precision.HIGH
eps = 1e-06
COEF = tuple(c / 6561.0 for c in (6560.0, 6544.0, 6432.0, 5984.0, 4864.0, 3072.0, 1280.0, 256.0))


def split(x):
    big = x.astype(bf16)
    return big, (x - big.astype(f32)).astype(bf16)


def dot1(a, b):
    return jnp.dot(a, b, preferred_element_type=f32)


def dot3(a, b):
    return dot1(a[0], b[0]) + (dot1(a[0], b[1]) + dot1(a[1], b[0]))


def sweep(gram, row, column):
    on_diag = row == column
    only = jnp.where(on_diag, gram, 0.0)
    d_row = jnp.sum(only, axis=0, keepdims=True)
    d_col = jnp.sum(only, axis=1, keepdims=True)
    ratio = gram / (d_col + d_row + eps)
    raw = jnp.where(row < column, ratio, jnp.where(row > column, -ratio, 0.0))
    scale = jnp.maximum(jnp.sqrt(jnp.sum(raw * raw, keepdims=True)), 1.0)
    skew = raw / scale
    parts = split(skew)
    a1 = dot1(parts[0], parts[0])
    a1b = a1.astype(bf16)
    a2 = dot1(a1b, a1b)
    a2b = a2.astype(bf16)
    a3 = dot1(a1b, a2b)
    a4 = dot1(a2b, a2b)
    low = COEF[5] * a1 + COEF[6] * a2 + COEF[7] * a3
    tail = dot1(a4.astype(bf16), low.astype(bf16))
    above = COEF[1] * a1 + COEF[2] * a2 + COEF[3] * a3 + (COEF[4] * a4 + tail)
    factor = a1 - 2.0 * skew
    extra = above + COEF[0] * factor + dot1(factor.astype(bf16), above.astype(bf16))
    extra = extra + jnp.where(on_diag, COEF[0] - 1.0, 0.0)
    part = split(extra)
    half = gram + dot3(split(gram), part)
    return extra, part, half


def finish_turn(extra, half):
    return half + dot3(split(extra.T), split(half))


def rotate_kernel(flag_ref, top_ref, cross_ref, low_ref, vs_ref, vk_ref, extra_ref, half_ref, g_ref):
    block = top_ref.shape[0]
    width = 2 * block
    g_ref[:block, :block] = top_ref[...]
    g_ref[:block, block:] = cross_ref[...]
    g_ref[block:, :block] = cross_ref[...].T
    g_ref[block:, block:] = low_ref[...]
    row = lax.broadcasted_iota(jnp.int32, (width, width), 0)
    column = lax.broadcasted_iota(jnp.int32, (width, width), 1)
    total = None
    for turn in range(SWEEPS):
        extra, part, half = sweep(g_ref[...], row, column)
        if total is None:
            total, total_part = extra, part
        else:
            total = total + extra + dot1(total_part[0], part[0])
            total_part = split(total)
        if turn + 1 < SWEEPS:
            g_ref[...] = finish_turn(extra, half)
    extra_ref[...] = extra
    half_ref[...] = half
    rotation = total + jnp.where(row == column, 1.0, 0.0)
    flag = flag_ref[0] == 1
    left = rotation[:, :block]
    right = rotation[:, block:]
    vs_ref[...] = jnp.where(flag, right, left)
    vk_ref[...] = jnp.where(flag, left, right)


def rotate(flag, top, cross, low):
    block = top.shape[0]
    width = 2 * block
    vmem = pl.BlockSpec(memory_space=pltpu.VMEM)
    shape = jax.ShapeDtypeStruct
    return pl.pallas_call(
        rotate_kernel,
        out_shape=(
            shape((width, block), f32),
            shape((width, block), f32),
            shape((width, width), f32),
            shape((width, width), f32),
        ),
        in_specs=[pl.BlockSpec(memory_space=pltpu.SMEM), vmem, vmem, vmem],
        out_specs=(vmem,) * 4,
        scratch_shapes=[pltpu.VMEM((width, width), f32)],
        compiler_params=pltpu.CompilerParams(vmem_limit_bytes=40 * 1024 * 1024),
        name="rotate",
    )(flag, top, cross, low)


def tall(first, second):
    def one(a, b):
        return lax.dot_general(a, b, (((0,), (0,)), ((), ())), preferred_element_type=f32)

    return one(first[0], second[0]) + (one(first[0], second[1]) + one(first[1], second[0]))


def remote(src, dst, send, recv, where):
    return pltpu.make_async_remote_copy(
        src_ref=src, dst_ref=dst, send_sem=send, recv_sem=recv, device_id=where, device_id_type=MESH
    )


def turn_stats(extra_ref, half_ref, turned_ref, block):
    turned_ref[...] = finish_turn(extra_ref[...], half_ref[...])
    off = turned_ref[:block, block:]
    row = lax.broadcasted_iota(jnp.int32, turned_ref.shape, 0)
    column = lax.broadcasted_iota(jnp.int32, turned_ref.shape, 1)
    only = jnp.where(row == column, turned_ref[...], 0.0)
    cross_sq = jnp.sum(off * off, keepdims=True)
    diag_sq = jnp.sum(only * only, keepdims=True)
    lane = lax.broadcasted_iota(jnp.int32, (1, 128), 1)
    return jnp.where(lane == 0, cross_sq, jnp.where(lane == 1, diag_sq, 0.0))


def step_kernel(cols, rows, chunk, flag_ref, pair_ref, vs_ref, vk_ref, extra_ref, half_ref,
                pair_out, cross_out, top_out, low_out, stat_out,
                send, turned, pass_gram, local, got,
                sem_s, sem_r, sem_gs, sem_gr, sem_as, sem_ar, sem_bs, sem_br):
    block = vs_ref.shape[1]
    pieces = block // chunk
    col = lax.axis_index("col")
    me = lax.axis_index("row")
    right = lax.rem(col + 1, cols)
    left = lax.rem(col + cols - 1, cols)
    barrier = pltpu.get_barrier_semaphore()
    for place in (left, right):
        pl.semaphore_signal(barrier, inc=1, device_id={"col": place}, device_id_type=MESH)
    for k in range(1, rows):
        pl.semaphore_signal(barrier, inc=1, device_id={"row": lax.rem(me + k, rows)}, device_id_type=MESH)
    part = split(pair_ref[...])
    passes = []
    for j in range(pieces):
        at = slice(j * chunk, (j + 1) * chunk)
        send[j] = dot3(part, split(vs_ref[:, at]))
        if j == 0:
            pl.semaphore_wait(barrier, rows + 1)
        copy = remote(send.at[j], pair_out.at[:, block + j * chunk : block + (j + 1) * chunk],
                      sem_s.at[j], sem_r.at[j], {"col": right})
        copy.start()
        passes.append(copy)
    keep = dot3(part, split(vk_ref[...]))
    pair_out[:, :block] = keep
    stat_out[...] = jnp.broadcast_to(turn_stats(extra_ref, half_ref, turned, block), stat_out.shape)
    flag = flag_ref[0] == 1
    top = turned[:block, :block]
    low = turned[block:, block:]
    top_out[...] = jnp.where(flag, top, low)
    pass_gram[...] = jnp.where(flag, low, top)
    gram_pass = remote(pass_gram, low_out, sem_gs, sem_gr, {"col": right})
    gram_pass.start()
    keep_part = split(keep)
    rows_each = block // rows
    first = []
    for j in range(pieces):
        passes[j].wait_recv()
        got_block = pair_out[:, block + j * chunk : block + (j + 1) * chunk]
        local[j] = tall(keep_part, split(got_block))
        for k in range(1, rows):
            peer = lax.rem(me + k, rows)
            theirs = pl.ds(pl.multiple_of(peer * rows_each, rows_each), rows_each)
            copy = remote(local.at[j, theirs], got.at[j, k - 1],
                          sem_as.at[j, k - 1], sem_ar.at[j, k - 1], {"row": peer})
            copy.start()
            first.append(copy)
    mine = pl.ds(pl.multiple_of(me * rows_each, rows_each), rows_each)
    second = []
    for j in range(pieces):
        at = slice(j * chunk, (j + 1) * chunk)
        for k in range(1, rows):
            first[j * (rows - 1) + k - 1].wait_recv()
        total = local[j, mine, :]
        for k in range(1, rows):
            total = total + got[j, k - 1]
        cross_out[mine, at] = total
        for k in range(1, rows):
            spot = cross_out.at[mine, at]
            copy = remote(spot, spot, sem_bs.at[j, k - 1], sem_br.at[j, k - 1],
                          {"row": lax.rem(me + k, rows)})
            copy.start()
            second.append(copy)
    for copy in second:
        copy.wait()
    for copy in first + passes:
        copy.wait_send()
    gram_pass.wait()


def step_call(flag, pair, vs, vk, extra, half, number):
    tall_rows, width = pair.shape
    block = width // 2
    chunk = min(block, 128)
    pieces = block // chunk
    cols, rows = lax.axis_size("col"), lax.axis_size("row")
    vmem = pl.BlockSpec(memory_space=pltpu.VMEM)
    shape = jax.ShapeDtypeStruct
    dma = pltpu.SemaphoreType.DMA
    return pl.pallas_call(
        functools.partial(step_kernel, cols, rows, chunk),
        out_shape=(
            shape((tall_rows, width), f32),
            shape((block, block), f32),
            shape((block, block), f32),
            shape((block, block), f32),
            shape((8, 128), f32),
        ),
        in_specs=[pl.BlockSpec(memory_space=pltpu.SMEM)] + [vmem] * 5,
        out_specs=(vmem,) * 5,
        scratch_shapes=[
            pltpu.VMEM((pieces, tall_rows, chunk), f32),
            pltpu.VMEM((width, width), f32),
            pltpu.VMEM((block, block), f32),
            pltpu.VMEM((pieces, block, chunk), f32),
            pltpu.VMEM((pieces, rows - 1, block // rows, chunk), f32),
            dma((pieces,)), dma((pieces,)), dma, dma,
            dma((pieces, rows - 1)), dma((pieces, rows - 1)),
            dma((pieces, rows - 1)), dma((pieces, rows - 1)),
        ],
        compiler_params=pltpu.CompilerParams(
            collective_id=number, has_side_effects=True, vmem_limit_bytes=50 * 1024 * 1024
        ),
        name="step",
    )(flag, pair, vs, vk, extra, half)


def last_kernel(cols, chunk, before_ref, pair_ref, vs_ref, vk_ref, extra_ref, half_ref,
                pair_out, sums_out, send, turned, mine, got, sem_s, sem_r, sem_ts, sem_tr):
    block = vs_ref.shape[1]
    pieces = block // chunk
    col = lax.axis_index("col")
    barrier = pltpu.get_barrier_semaphore()
    for k in range(1, cols):
        pl.semaphore_signal(barrier, inc=1, device_id={"col": lax.rem(col + k, cols)}, device_id_type=MESH)
    part = split(pair_ref[...])
    copies = []
    for j in range(pieces):
        at = slice(j * chunk, (j + 1) * chunk)
        send[j] = dot3(part, split(vs_ref[:, at]))
        if j == 0:
            pl.semaphore_wait(barrier, cols - 1)
        copy = remote(send.at[j], pair_out.at[:, block + j * chunk : block + (j + 1) * chunk],
                      sem_s.at[j], sem_r.at[j], {"col": lax.rem(col + 1, cols)})
        copy.start()
        copies.append(copy)
        if j == 0:
            stat = turn_stats(extra_ref, half_ref, turned, block)
            line = lax.broadcasted_iota(jnp.int32, before_ref.shape, 0)
            tile = jnp.where(line == STEPS - 1, stat, before_ref[...])
            mine[...] = tile
            got[col] = tile
            for k in range(1, cols):
                copy = remote(mine, got.at[col], sem_ts.at[k - 1], sem_tr.at[k - 1],
                              {"col": lax.rem(col + k, cols)})
                copy.start()
                copies.append(copy)
    pair_out[:, :block] = dot3(part, split(vk_ref[...]))
    for copy in copies:
        copy.wait()
    total = got[0]
    for k in range(1, cols):
        total = total + got[k]
    sums_out[...] = total


def last_call(before, pair, vs, vk, extra, half, number):
    tall_rows, width = pair.shape
    block = width // 2
    chunk = min(block, 128)
    pieces = block // chunk
    cols = lax.axis_size("col")
    vmem = pl.BlockSpec(memory_space=pltpu.VMEM)
    shape = jax.ShapeDtypeStruct
    dma = pltpu.SemaphoreType.DMA
    return pl.pallas_call(
        functools.partial(last_kernel, cols, chunk),
        out_shape=(shape((tall_rows, width), f32), shape(before.shape, f32)),
        in_specs=[vmem] * 6,
        out_specs=(vmem,) * 2,
        scratch_shapes=[
            pltpu.VMEM((pieces, tall_rows, chunk), f32),
            pltpu.VMEM((width, width), f32),
            pltpu.VMEM(before.shape, f32),
            pltpu.VMEM((cols,) + before.shape, f32),
            dma((pieces,)), dma((pieces,)), dma((cols - 1,)), dma((cols - 1,)),
        ],
        compiler_params=pltpu.CompilerParams(
            collective_id=number, has_side_effects=True, vmem_limit_bytes=50 * 1024 * 1024
        ),
        name="last",
    )(before, pair, vs, vk, extra, half)


def greet(axis, count, me):
    barrier = pltpu.get_barrier_semaphore()
    for k in range(1, count):
        pl.semaphore_signal(
            barrier, inc=1, device_id={axis: lax.rem(me + k, count)}, device_id_type=MESH
        )
    pl.semaphore_wait(barrier, count - 1)


def sum_kernel(axis, count, x_ref, out_ref, got, send_a, recv_a, send_b, recv_b):
    me = lax.axis_index(axis)
    rows = x_ref.shape[0] // count
    greet(axis, count, me)
    mine = pl.ds(pl.multiple_of(me * rows, rows), rows)
    copies = []
    for k in range(1, count):
        peer = lax.rem(me + k, count)
        theirs = pl.ds(pl.multiple_of(peer * rows, rows), rows)
        copy = pltpu.make_async_remote_copy(
            src_ref=x_ref.at[theirs],
            dst_ref=got.at[k - 1],
            send_sem=send_a.at[k - 1],
            recv_sem=recv_a.at[k - 1],
            device_id={axis: peer},
            device_id_type=MESH,
        )
        copy.start()
        copies.append(copy)
    for copy in copies:
        copy.wait()
    total = x_ref[mine, :]
    for k in range(1, count):
        total = total + got[k - 1]
    out_ref[mine, :] = total
    copies = []
    for k in range(1, count):
        peer = lax.rem(me + k, count)
        copy = pltpu.make_async_remote_copy(
            src_ref=out_ref.at[mine],
            dst_ref=out_ref.at[mine],
            send_sem=send_b.at[k - 1],
            recv_sem=recv_b.at[k - 1],
            device_id={axis: peer},
            device_id_type=MESH,
        )
        copy.start()
        copies.append(copy)
    for copy in copies:
        copy.wait()


def sum_over(x, axis, number):
    count = lax.axis_size(axis)
    rows, width = x.shape
    vmem = pl.BlockSpec(memory_space=pltpu.VMEM)
    return pl.pallas_call(
        functools.partial(sum_kernel, axis, count),
        out_shape=jax.ShapeDtypeStruct((rows, width), f32),
        in_specs=[vmem],
        out_specs=vmem,
        scratch_shapes=[pltpu.VMEM((count - 1, rows // count, width), f32)]
        + [pltpu.SemaphoreType.DMA((count - 1,))] * 4,
        compiler_params=pltpu.CompilerParams(
            collective_id=number, has_side_effects=True, vmem_limit_bytes=16 * 1024 * 1024
        ),
        name="row_sum",
    )(x)


def local_product(first, second):
    return lax.dot_general(
        first, second, (((0,), (0,)), ((), ())), precision=high, preferred_element_type=f32
    )


def on_device(matrix, plan):
    block = matrix.shape[1] // 2
    position = lax.axis_index("col")
    picker = jnp.arange(plan.shape[1], dtype=jnp.int32) == position
    flags = jnp.sum(jnp.where(picker[None, :], plan, 0), axis=1)
    keep, received = matrix[:, :block], matrix[:, block:]
    upper = local_product(keep, matrix)
    lower = local_product(received, received)
    packed = sum_over(jnp.concatenate([upper[:, :block], upper[:, block:], lower], axis=0), "row", 0)
    top, cross, low = packed[:block], packed[block : 2 * block], packed[2 * block :]
    pair = matrix
    stats = []
    for step in range(STEPS):
        flag = flags[step : step + 1]
        vs, vk, extra, half = rotate(flag, top, cross, low)
        if step + 1 < STEPS:
            pair, cross, top, low, stat = step_call(flag, pair, vs, vk, extra, half, step + 1)
            stats.append(stat[:1])
    before = jnp.concatenate(stats + [jnp.zeros((8 - len(stats), 128), f32)], axis=0)
    pair, sums = last_call(before, pair, vs, vk, extra, half, STEPS)
    return (pair, jnp.log(sums[:STEPS, 0] / sums[:STEPS, 1]))


def solution(mesh):
    in_specs = (P("row", "col"), P())
    out_specs = (P("row", "col"), P())
    return jax.shard_map(
        on_device, mesh=mesh, in_specs=in_specs, out_specs=out_specs, check_vma=False
    )
```

```python
import functools

import jax
import jax.numpy as jnp
from jax import lax
from jax.experimental import pallas as pl
from jax.experimental.pallas import tpu as pltpu
from jax.sharding import PartitionSpec as P

SWEEPS = 2
STEPS = 3
MESH = pl.DeviceIdType.MESH
f32 = jnp.float32
bf16 = jnp.bfloat16
eps = 1e-06
COEF = tuple(c / 6561.0 for c in (6560.0, 6544.0, 6432.0, 5984.0, 4864.0, 3072.0, 1280.0, 256.0))


def split(x):
    big = x.astype(bf16)
    return big, (x - big.astype(f32)).astype(bf16)


def dot1(a, b):
    return jnp.dot(a, b, preferred_element_type=f32)


def dot3(a, b):
    return dot1(a[0], b[0]) + (dot1(a[0], b[1]) + dot1(a[1], b[0]))


def sweep(gram, row, column):
    on_diag = row == column
    only = jnp.where(on_diag, gram, 0.0)
    d_row = jnp.sum(only, axis=0, keepdims=True)
    d_col = jnp.sum(only, axis=1, keepdims=True)
    ratio = gram / (d_col + d_row + eps)
    raw = jnp.where(row < column, ratio, jnp.where(row > column, -ratio, 0.0))
    scale = jnp.maximum(jnp.sqrt(jnp.sum(raw * raw, keepdims=True)), 1.0)
    skew = raw / scale
    parts = split(skew)
    a1 = dot1(parts[0], parts[0])
    a1b = a1.astype(bf16)
    a2 = dot1(a1b, a1b)
    a2b = a2.astype(bf16)
    a3 = dot1(a1b, a2b)
    a4 = dot1(a2b, a2b)
    low = COEF[5] * a1 + COEF[6] * a2 + COEF[7] * a3
    tail = dot1(a4.astype(bf16), low.astype(bf16))
    above = COEF[1] * a1 + COEF[2] * a2 + COEF[3] * a3 + (COEF[4] * a4 + tail)
    factor = a1 - 2.0 * skew
    extra = above + COEF[0] * factor + dot1(factor.astype(bf16), above.astype(bf16))
    extra = extra + jnp.where(on_diag, COEF[0] - 1.0, 0.0)
    part = split(extra)
    half = gram + dot3(split(gram), part)
    return extra, part, half


def finish_turn(extra, half):
    return half + dot3(split(extra.T), split(half))


def rotate_kernel(flag_ref, top_ref, cross_ref, low_ref, vs_ref, vk_ref, extra_ref, half_ref, g_ref, total_ref):
    block = top_ref.shape[0]
    width = 2 * block
    g_ref[:block, :block] = top_ref[...]
    g_ref[:block, block:] = cross_ref[...]
    g_ref[block:, :block] = cross_ref[...].T
    g_ref[block:, block:] = low_ref[...]
    row = lax.broadcasted_iota(jnp.int32, (width, width), 0)
    column = lax.broadcasted_iota(jnp.int32, (width, width), 1)
    total_ref[...] = jnp.zeros_like(total_ref)

    @pl.loop(0, SWEEPS)
    def _(turn):
        extra, part, half = sweep(g_ref[...], row, column)
        total = total_ref[...]
        total_ref[...] = total + extra + dot1(total.astype(bf16), part[0])
        extra_ref[...] = extra
        half_ref[...] = half

        @pl.when(turn + 1 < SWEEPS)
        def _():
            g_ref[...] = finish_turn(extra_ref[...], half_ref[...])

    total = total_ref[...]
    rotation = total + jnp.where(row == column, 1.0, 0.0)
    flag = flag_ref[0] == 1
    left = rotation[:, :block]
    right = rotation[:, block:]
    vs_ref[...] = jnp.where(flag, right, left)
    vk_ref[...] = jnp.where(flag, left, right)


def rotate(flag, top, cross, low):
    block = top.shape[0]
    width = 2 * block
    vmem = pl.BlockSpec(memory_space=pltpu.VMEM)
    shape = jax.ShapeDtypeStruct
    return pl.pallas_call(
        rotate_kernel,
        out_shape=(
            shape((width, block), f32),
            shape((width, block), f32),
            shape((width, width), f32),
            shape((width, width), f32),
        ),
        in_specs=[pl.BlockSpec(memory_space=pltpu.SMEM), vmem, vmem, vmem],
        out_specs=(vmem,) * 4,
        scratch_shapes=[pltpu.VMEM((width, width), f32)] * 2,
        compiler_params=pltpu.CompilerParams(vmem_limit_bytes=40 * 1024 * 1024),
        name="rotate",
    )(flag, top, cross, low)


def tall(first, second):
    def one(a, b):
        return lax.dot_general(a, b, (((0,), (0,)), ((), ())), preferred_element_type=f32)

    return one(first[0], second[0]) + (one(first[0], second[1]) + one(first[1], second[0]))


def remote(src, dst, send, recv, where):
    return pltpu.make_async_remote_copy(
        src_ref=src, dst_ref=dst, send_sem=send, recv_sem=recv, device_id=where, device_id_type=MESH
    )


def turn_stats(extra_ref, half_ref, turned_ref, block):
    turned_ref[...] = finish_turn(extra_ref[...], half_ref[...])
    off = turned_ref[:block, block:]
    row = lax.broadcasted_iota(jnp.int32, turned_ref.shape, 0)
    column = lax.broadcasted_iota(jnp.int32, turned_ref.shape, 1)
    only = jnp.where(row == column, turned_ref[...], 0.0)
    cross_sq = jnp.sum(off * off, keepdims=True)
    diag_sq = jnp.sum(only * only, keepdims=True)
    lane = lax.broadcasted_iota(jnp.int32, (1, 128), 1)
    return jnp.where(lane == 0, cross_sq, jnp.where(lane == 1, diag_sq, 0.0))


def step_kernel(cols, rows, chunk, flag_ref, pair_ref, vs_ref, vk_ref, extra_ref, half_ref,
                pair_out, cross_out, top_out, low_out, stat_out,
                send, turned, pass_gram, local, got,
                sem_s, sem_r, sem_gs, sem_gr, sem_as, sem_ar, sem_bs, sem_br):
    block = vs_ref.shape[1]
    pieces = block // chunk
    col = lax.axis_index("col")
    me = lax.axis_index("row")
    right = lax.rem(col + 1, cols)
    left = lax.rem(col + cols - 1, cols)
    barrier = pltpu.get_barrier_semaphore()
    for place in (left, right):
        pl.semaphore_signal(barrier, inc=1, device_id={"col": place}, device_id_type=MESH)
    for k in range(1, rows):
        pl.semaphore_signal(barrier, inc=1, device_id={"row": lax.rem(me + k, rows)}, device_id_type=MESH)
    part = split(pair_ref[...])
    passes = []
    for j in range(pieces):
        at = slice(j * chunk, (j + 1) * chunk)
        send[j] = dot3(part, split(vs_ref[:, at]))
        if j == 0:
            pl.semaphore_wait(barrier, rows + 1)
        copy = remote(send.at[j], pair_out.at[:, block + j * chunk : block + (j + 1) * chunk],
                      sem_s.at[j], sem_r.at[j], {"col": right})
        copy.start()
        passes.append(copy)
    keep = dot3(part, split(vk_ref[...]))
    pair_out[:, :block] = keep
    stat_out[...] = jnp.broadcast_to(turn_stats(extra_ref, half_ref, turned, block), stat_out.shape)
    flag = flag_ref[0] == 1
    top = turned[:block, :block]
    low = turned[block:, block:]
    top_out[...] = jnp.where(flag, top, low)
    pass_gram[...] = jnp.where(flag, low, top)
    gram_pass = remote(pass_gram, low_out, sem_gs, sem_gr, {"col": right})
    gram_pass.start()
    keep_part = split(keep)
    rows_each = block // rows
    first = []
    for j in range(pieces):
        passes[j].wait_recv()
        got_block = pair_out[:, block + j * chunk : block + (j + 1) * chunk]
        local[j] = tall(keep_part, split(got_block))
        for k in range(1, rows):
            peer = lax.rem(me + k, rows)
            theirs = pl.ds(pl.multiple_of(peer * rows_each, rows_each), rows_each)
            copy = remote(local.at[j, theirs], got.at[j, k - 1],
                          sem_as.at[j, k - 1], sem_ar.at[j, k - 1], {"row": peer})
            copy.start()
            first.append(copy)
    mine = pl.ds(pl.multiple_of(me * rows_each, rows_each), rows_each)
    second = []
    for j in range(pieces):
        at = slice(j * chunk, (j + 1) * chunk)
        for k in range(1, rows):
            first[j * (rows - 1) + k - 1].wait_recv()
        total = local[j, mine, :]
        for k in range(1, rows):
            total = total + got[j, k - 1]
        cross_out[mine, at] = total
        for k in range(1, rows):
            spot = cross_out.at[mine, at]
            copy = remote(spot, spot, sem_bs.at[j, k - 1], sem_br.at[j, k - 1],
                          {"row": lax.rem(me + k, rows)})
            copy.start()
            second.append(copy)
    for copy in second:
        copy.wait()
    for copy in first + passes:
        copy.wait_send()
    gram_pass.wait()


def step_call(flag, pair, vs, vk, extra, half, number):
    tall_rows, width = pair.shape
    block = width // 2
    chunk = min(block, 128)
    pieces = block // chunk
    cols, rows = lax.axis_size("col"), lax.axis_size("row")
    vmem = pl.BlockSpec(memory_space=pltpu.VMEM)
    shape = jax.ShapeDtypeStruct
    dma = pltpu.SemaphoreType.DMA
    return pl.pallas_call(
        functools.partial(step_kernel, cols, rows, chunk),
        out_shape=(
            shape((tall_rows, width), f32),
            shape((block, block), f32),
            shape((block, block), f32),
            shape((block, block), f32),
            shape((8, 128), f32),
        ),
        in_specs=[pl.BlockSpec(memory_space=pltpu.SMEM)] + [vmem] * 5,
        out_specs=(vmem,) * 5,
        scratch_shapes=[
            pltpu.VMEM((pieces, tall_rows, chunk), f32),
            pltpu.VMEM((width, width), f32),
            pltpu.VMEM((block, block), f32),
            pltpu.VMEM((pieces, block, chunk), f32),
            pltpu.VMEM((pieces, rows - 1, block // rows, chunk), f32),
            dma((pieces,)), dma((pieces,)), dma, dma,
            dma((pieces, rows - 1)), dma((pieces, rows - 1)),
            dma((pieces, rows - 1)), dma((pieces, rows - 1)),
        ],
        compiler_params=pltpu.CompilerParams(
            collective_id=number, has_side_effects=True, vmem_limit_bytes=50 * 1024 * 1024
        ),
        name="step",
    )(flag, pair, vs, vk, extra, half)


def last_kernel(cols, chunk, before_ref, pair_ref, vs_ref, vk_ref, extra_ref, half_ref,
                pair_out, sums_out, send, turned, mine, got, sem_s, sem_r, sem_ts, sem_tr):
    block = vs_ref.shape[1]
    pieces = block // chunk
    col = lax.axis_index("col")
    barrier = pltpu.get_barrier_semaphore()
    for k in range(1, cols):
        pl.semaphore_signal(barrier, inc=1, device_id={"col": lax.rem(col + k, cols)}, device_id_type=MESH)
    part = split(pair_ref[...])
    copies = []
    for j in range(pieces):
        at = slice(j * chunk, (j + 1) * chunk)
        send[j] = dot3(part, split(vs_ref[:, at]))
        if j == 0:
            pl.semaphore_wait(barrier, cols - 1)
        copy = remote(send.at[j], pair_out.at[:, block + j * chunk : block + (j + 1) * chunk],
                      sem_s.at[j], sem_r.at[j], {"col": lax.rem(col + 1, cols)})
        copy.start()
        copies.append(copy)
        if j == 0:
            stat = turn_stats(extra_ref, half_ref, turned, block)
            line = lax.broadcasted_iota(jnp.int32, before_ref.shape, 0)
            tile = jnp.where(line == STEPS - 1, stat, before_ref[...])
            mine[...] = tile
            got[col] = tile
            for k in range(1, cols):
                copy = remote(mine, got.at[col], sem_ts.at[k - 1], sem_tr.at[k - 1],
                              {"col": lax.rem(col + k, cols)})
                copy.start()
                copies.append(copy)
    pair_out[:, :block] = dot3(part, split(vk_ref[...]))
    for copy in copies:
        copy.wait()
    total = got[0]
    for k in range(1, cols):
        total = total + got[k]
    sums_out[...] = total


def last_call(before, pair, vs, vk, extra, half, number):
    tall_rows, width = pair.shape
    block = width // 2
    chunk = min(block, 128)
    pieces = block // chunk
    cols = lax.axis_size("col")
    vmem = pl.BlockSpec(memory_space=pltpu.VMEM)
    shape = jax.ShapeDtypeStruct
    dma = pltpu.SemaphoreType.DMA
    return pl.pallas_call(
        functools.partial(last_kernel, cols, chunk),
        out_shape=(shape((tall_rows, width), f32), shape(before.shape, f32)),
        in_specs=[vmem] * 6,
        out_specs=(vmem,) * 2,
        scratch_shapes=[
            pltpu.VMEM((pieces, tall_rows, chunk), f32),
            pltpu.VMEM((width, width), f32),
            pltpu.VMEM(before.shape, f32),
            pltpu.VMEM((cols,) + before.shape, f32),
            dma((pieces,)), dma((pieces,)), dma((cols - 1,)), dma((cols - 1,)),
        ],
        compiler_params=pltpu.CompilerParams(
            collective_id=number, has_side_effects=True, vmem_limit_bytes=50 * 1024 * 1024
        ),
        name="last",
    )(before, pair, vs, vk, extra, half)


def gram_kernel(rows, chunk, pair_ref, top_ref, cross_ref, low_ref, local, got,
                sem_as, sem_ar, sem_bs, sem_br):
    block = top_ref.shape[0]
    me = lax.axis_index("row")
    barrier = pltpu.get_barrier_semaphore()
    for k in range(1, rows):
        pl.semaphore_signal(barrier, inc=1, device_id={"row": lax.rem(me + k, rows)}, device_id_type=MESH)
    rows_each = block // rows
    mine = pl.ds(pl.multiple_of(me * rows_each, rows_each), rows_each)
    jobs = []
    for out, first, second in ((top_ref, 0, 0), (cross_ref, 0, block), (low_ref, block, block)):
        for start in range(0, block, chunk):
            jobs.append((out, first, second + start, start))
    halves = {at: split(pair_ref[:, at : at + block]) for at in (0, block)}
    scatter = []
    for j, (out, first, second, start) in enumerate(jobs):
        local[j] = tall(halves[first], split(pair_ref[:, second : second + chunk]))
        if j == 0:
            pl.semaphore_wait(barrier, rows - 1)
        for k in range(1, rows):
            peer = lax.rem(me + k, rows)
            theirs = pl.ds(pl.multiple_of(peer * rows_each, rows_each), rows_each)
            copy = remote(local.at[j, theirs], got.at[j, k - 1],
                          sem_as.at[j, k - 1], sem_ar.at[j, k - 1], {"row": peer})
            copy.start()
            scatter.append(copy)
    gather = []
    for j, (out, first, second, start) in enumerate(jobs):
        total = local[j, mine, :]
        for k in range(1, rows):
            scatter[j * (rows - 1) + k - 1].wait_recv()
            total = total + got[j, k - 1]
        out[mine, start : start + chunk] = total
        for k in range(1, rows):
            spot = out.at[mine, start : start + chunk]
            copy = remote(spot, spot, sem_bs.at[j, k - 1], sem_br.at[j, k - 1],
                          {"row": lax.rem(me + k, rows)})
            copy.start()
            gather.append(copy)
    for copy in gather:
        copy.wait()
    for copy in scatter:
        copy.wait_send()


def gram_call(pair, number):
    block = pair.shape[1] // 2
    chunk = min(block, 128)
    pieces = 3 * block // chunk
    rows = lax.axis_size("row")
    vmem = pl.BlockSpec(memory_space=pltpu.VMEM)
    dma = pltpu.SemaphoreType.DMA
    return pl.pallas_call(
        functools.partial(gram_kernel, rows, chunk),
        out_shape=(jax.ShapeDtypeStruct((block, block), f32),) * 3,
        in_specs=[vmem],
        out_specs=(vmem,) * 3,
        scratch_shapes=[
            pltpu.VMEM((pieces, block, chunk), f32),
            pltpu.VMEM((pieces, rows - 1, block // rows, chunk), f32),
        ]
        + [dma((pieces, rows - 1))] * 4,
        compiler_params=pltpu.CompilerParams(
            collective_id=number, has_side_effects=True, vmem_limit_bytes=40 * 1024 * 1024
        ),
        name="gram",
    )(pair)


def on_device(matrix, plan):
    position = lax.axis_index("col")
    picker = jnp.arange(plan.shape[1], dtype=jnp.int32) == position
    flags = jnp.sum(jnp.where(picker[None, :], plan, 0), axis=1)
    top, cross, low = gram_call(matrix, 0)
    pair = matrix
    stats = []
    for step in range(STEPS):
        flag = flags[step : step + 1]
        vs, vk, extra, half = rotate(flag, top, cross, low)
        if step + 1 < STEPS:
            pair, cross, top, low, stat = step_call(flag, pair, vs, vk, extra, half, step + 1)
            stats.append(stat[:1])
    before = jnp.concatenate(stats + [jnp.zeros((8 - len(stats), 128), f32)], axis=0)
    pair, sums = last_call(before, pair, vs, vk, extra, half, STEPS)
    return (pair, jnp.log(sums[:STEPS, 0] / sums[:STEPS, 1]))


def solution(mesh):
    in_specs = (P("row", "col"), P())
    out_specs = (P("row", "col"), P())
    return jax.shard_map(
        on_device, mesh=mesh, in_specs=in_specs, out_specs=out_specs, check_vma=False
    )
```
